32 devices in a mesh: tok: 2 (over x), fin: 4 (over y, core), fout: 4 (over z).
Axes of the slice: x: 2, y: 2, z: 4, core: 2. Of those that a mesh axis runs over, the one named last changes fastest.
Arguments:
- acts: float32 [1024, 12288], P('tok', 'fin'), may hold values from -6 to 6
- weight: float32 [12288, 12288], P(('fin', 'tok'), 'fout'), may hold values from -0.0546875 to 0.0546875
- grad_out: float32 [1024, 12288], P(('tok', 'fin'), 'fout'), may hold values from -6 to 6
Outputs:
- outputs: float32 [1024, 12288], P(('tok', 'fin'), 'fout')
- grad_acts: float32 [1024, 12288], P(('tok', 'fout'), 'fin')
- grad_weight: float32 [12288, 12288], P(('fin', 'tok'), 'fout')
The draws below stay inside these ranges and needn't reach their ends.
All inputs are finite; a program needn't handle non-finite values.
Results may differ from the reference program's by a relative error of at most 0.000075.
Values sent between devices are 32-bit elements; how exact they have to be, the bound alone decides.
No kernel may reach another device: no remote copies, remote signals or barrier semaphores. Data moves between devices by JAX's collectives and lax.ppermute only.
A program may use at most 192 MiB of HBM per device.

```python
import jax
import jax.numpy as jnp
from jax import lax

D = 12288
TOKENS = 1024


def block_scale(stream_key, extent, split, least, top_value):
    factor_of = 1.0
    for position, shards_of in split:
        steps = jax.random.uniform(jax.random.fold_in(jax.random.fold_in(stream_key, 6), position), (shards_of,), jnp.float32, least / len(split), top_value / len(split))
        factor_of = factor_of * jnp.repeat(jnp.exp(steps), extent[position] // shards_of).reshape((-1,) + (1,) * (len(extent) - 1 - position))
    return factor_of


def bell_draw(rng, shape, deviation, limit, pieces=(), dtype=jnp.bfloat16):
    loudness = block_scale(rng, shape, pieces, -0.22, 0.18) if pieces else 1.0
    result = jax.random.normal(rng, shape, jnp.float32) * deviation * loudness
    return jnp.minimum(jnp.maximum(result, -limit), limit).astype(dtype)


def setup_inputs(seed: int = 0) -> dict:
    streams_of = jax.random.split(jax.random.key(seed), 4)
    return {
        "acts": bell_draw(streams_of[0], (TOKENS, D), 1.0, 6.0, ((0, 2), (1, 4)), jnp.float32),
        "weight": bell_draw(streams_of[1], (D, D), D ** -0.5, 0.0546875, ((0, 8), (1, 4)), jnp.float32),
        "grad_out": bell_draw(streams_of[2], (TOKENS, D), 1.0, 6.0, ((0, 8), (1, 4)), jnp.float32),
    }


def reference(acts, weight, grad_out):
    high = lax.Precision.HIGHEST
    outputs = jnp.dot(acts, weight, precision=high, preferred_element_type=jnp.float32)
    grad_acts = jnp.dot(grad_out, weight.T, precision=high, preferred_element_type=jnp.float32)
    grad_weight = jnp.dot(acts.T, grad_out, precision=high, preferred_element_type=jnp.float32)
    return outputs, grad_acts, grad_weight
```

```python
import jax
import jax.numpy as jnp
from jax import lax
from jax.sharding import PartitionSpec as P


def product(left, right, left_dim, right_dim):
    return lax.dot_general(
        left,
        right,
        (((left_dim,), (right_dim,)), ((), ())),
        precision=lax.Precision.HIGH,
        preferred_element_type=jnp.float32,
    )


def swap(value, axis, bit):
    return lax.ppermute(value, axis, [(i, i ^ bit) for i in range(lax.axis_size(axis))])


def bits(size):
    return [1 << k for k in range(size.bit_length() - 1)]


def mirrored(size):
    width = size.bit_length() - 1
    return [int(format(k, "b").zfill(width)[::-1], 2) if width else 0 for k in range(size)]


def shards(acts, weight, grad_out):
    toks, fins, fouts = (lax.axis_size(name) for name in ("tok", "fin", "fout"))
    tok, fin, fout = (lax.axis_index(name) for name in ("tok", "fin", "fout"))
    block = grad_out.shape[0]
    depth = weight.shape[0]
    order = mirrored(fins)

    def acts_for(other):
        rows = [lax.dynamic_slice(acts, ((fin ^ r) * block, (tok ^ other) * depth), (block, depth)) for r in order]
        return jnp.concatenate(rows, 0)

    held = {(0, 0): grad_out}
    for bit in bits(toks):
        held.update({(s ^ bit, r): swap(v, "tok", bit) for (s, r), v in held.items()})
    for bit in reversed(bits(fins)):
        held.update({(s, r ^ bit): swap(v, "fin", bit) for (s, r), v in held.items()})
    own = [acts_for(s) for s in range(toks)]
    acts_of = [own[0]] + [swap(own[s], "tok", s) for s in range(1, toks)]
    grads_of = [jnp.concatenate([held[s, r] for r in order], 0) for s in range(toks)]

    parts = []
    for s in range(toks):
        part = product(acts_of[s], weight, 1, 0)
        for bit in bits(fins):
            half = part.shape[0] // 2
            part = part[:half] + swap(part[half:], "fin", bit)
        parts.append(part)
    outputs = parts[0]
    for s in range(1, toks):
        outputs = outputs + swap(parts[s], "tok", s)

    grad_acts = jnp.zeros((block, depth * toks), jnp.float32)
    turn = fin ^ fout
    for s in range(toks):
        part = product(grads_of[s], weight, 1, 1)
        for k, bit in enumerate(bits(fouts)):
            half = part.shape[0] // 2
            q = (turn >> k) & 1
            keep = lax.dynamic_slice(part, (q * half, 0), (half, depth))
            send = lax.dynamic_slice(part, ((1 - q) * half, 0), (half, depth))
            part = keep + swap(send, "fout", bit)
        if s:
            part = swap(part, "tok", s)
        grad_acts = lax.dynamic_update_slice(grad_acts, part, (0, (tok ^ s) * depth))

    grad_weight = product(jnp.concatenate(acts_of, 0), jnp.concatenate(grads_of, 0), 0, 0)
    return outputs, grad_acts, grad_weight


def solution(mesh):
    in_specs = (P("tok", "fin"), P(("fin", "tok"), "fout"), P(("tok", "fin"), "fout"))
    out_specs = (P(("tok", "fin"), "fout"), P(("tok", "fout"), "fin"), P(("fin", "tok"), "fout"))
    return jax.shard_map(shards, mesh=mesh, in_specs=in_specs, out_specs=out_specs, check_vma=False)
```

```python
import functools

import jax
import jax.numpy as jnp
from jax import lax
from jax.experimental import pallas as pl
from jax.experimental.pallas import tpu as pltpu
from jax.sharding import PartitionSpec as P


VMEM = 67043328


def swap(value, axis, bit):
    return lax.ppermute(value, axis, [(i, i ^ bit) for i in range(lax.axis_size(axis))])


def bits(size):
    return [1 << k for k in range(size.bit_length() - 1)]


def mirrored(size):
    width = size.bit_length() - 1
    return [int(format(k, "b").zfill(width)[::-1], 2) if width else 0 for k in range(size)]


def tile_of(extent, most):
    return next((t for t in range(most, 127, -128) if extent % t == 0), extent)


def split(value):
    high = value.astype(jnp.bfloat16)
    return high, (value - high.astype(jnp.float32)).astype(jnp.bfloat16)


def three_passes(lh, ll, rh, rl, left_dim, right_dim):
    def one(a, b):
        return lax.dot_general(a, b, (((left_dim,), (right_dim,)), ((), ())), preferred_element_type=jnp.float32)

    return one(lh, rh) + (one(lh, rl) + one(ll, rh))


def call(kernel, grid, in_specs, out_specs, out_shape, scratch, scalars, args, flops, aliases=None):
    return pl.pallas_call(
        kernel,
        grid_spec=pltpu.PrefetchScalarGridSpec(
            num_scalar_prefetch=1, grid=grid, in_specs=in_specs, out_specs=out_specs, scratch_shapes=scratch
        ),
        out_shape=out_shape,
        input_output_aliases=aliases or {},
        compiler_params=pltpu.CompilerParams(vmem_limit_bytes=VMEM),
        cost_estimate=pl.CostEstimate(flops=flops, bytes_accessed=2**24, transcendentals=0),
    )(scalars, *args)


def f32(*shape):
    return jax.ShapeDtypeStruct(shape, jnp.float32)


def bf16(*shape):
    return jax.ShapeDtypeStruct(shape, jnp.bfloat16)


def once(shape, index_map):
    return pl.BlockSpec(shape, index_map, pipeline_mode=pl.Buffered(1))


def copies_out(high, low, out_h, out_l, sems, count, block, source):
    made = []
    for k in range(count):
        rows = pl.ds(k * block, block)
        made.append(pltpu.make_async_copy(high.at[source(k), :], out_h.at[rows, :], sems.at[0, k]))
        made.append(pltpu.make_async_copy(low.at[source(k), :], out_l.at[rows, :], sems.at[1, k]))
    return made


def forward(scalars, pieces, specs, order, weight, block):
    depth, width = weight[0].shape
    count = len(order)
    tile = tile_of(width, 512)
    half = count // 2 * block
    steps = width // tile

    def kernel(s_ref, *refs):
        ins = refs[:count]
        wh_ref, wl_ref, keep, send, out_h, out_l, high, low, sems = refs[count:]

        def source(k):
            return pl.ds(order.index(k) * block, block)

        def copies():
            return copies_out(high, low, out_h, out_l, sems, count, block, source)

        @pl.when(pl.program_id(0) == 0)
        def _():
            for k in range(count):
                high[source(k), :], low[source(k), :] = split(ins[k][...])
            for copy in copies():
                copy.start()

        out = three_passes(high[...], low[...], wh_ref[...], wl_ref[...], 1, 0)
        keep[...] = out[:half]
        send[...] = out[half:]

        @pl.when(pl.program_id(0) == steps - 1)
        def _():
            for copy in copies():
                copy.wait()

    anywhere = pl.BlockSpec(memory_space=pl.ANY)
    part = pl.BlockSpec((half, tile), lambda i, s: (0, i))
    column = pl.BlockSpec((depth, tile), lambda i, s: (0, i))
    return call(kernel, (steps,), specs + [column, column], [part, part, anywhere, anywhere],
                [f32(half, width)] * 2 + [bf16(count * block, depth)] * 2,
                [pltpu.VMEM((count * block, depth), jnp.bfloat16)] * 2 + [pltpu.SemaphoreType.DMA((2, count))],
                scalars, pieces + list(weight), 6 * count * block * depth * width)


def placed(turn, size, k):
    at = k // size * size
    for level, bit in enumerate(bits(size)):
        at = at + (((k % size >> level) ^ (turn >> level)) & 1) * (size // 2 // bit)
    return at


def first(scalars, rows, specs, order, group, weight, block, source_of=None, column_of=None, others=()):
    halves = isinstance(weight, tuple)
    depth, width = weight[0].shape if halves else weight.shape
    count, size = len(order), len(group)
    tile = tile_of(width, 512)
    half, some = count // 2 * block, size // 2 * block
    steps = width // tile
    flat = [(s, r) for s, rows_of in others for r in rows_of]

    def kernel(s_ref, *refs):
        if flat:
            held, box, box_in, box_out = refs[0], *refs[-3:]
            packed = refs[-8 - len(others):-8]
            refs = refs[1:-8 - len(others)] + refs[-8:-3]

            def taken():
                return [pltpu.make_async_copy(
                    held.at[pl.ds(pl.multiple_of((s_ref[0] ^ r) * block, block), block),
                            pl.ds(pl.multiple_of(column_of(s, s_ref) * depth, depth), depth)],
                    box.at[k], box_in.at[k]) for k, (s, r) in enumerate(flat)]

            def given_out():
                made, k = [], 0
                for out, (_, rows_of) in zip(packed, others):
                    for at in range(len(rows_of)):
                        made.append(pltpu.make_async_copy(box.at[k], out.at[pl.ds(at * block, block), :], box_out.at[k]))
                        k += 1
                return made

            @pl.when(pl.program_id(0) == 0)
            def _():
                for copy in taken():
                    copy.start()

            @pl.when(pl.program_id(0) == min(1, steps - 1))
            def _():
                for come, go in zip(taken(), given_out()):
                    come.wait()
                    go.start()

            @pl.when(pl.program_id(0) == steps - 1)
            def _():
                for copy in given_out():
                    copy.wait()

        ins, grads, refs = refs[:count], refs[count:count + size], refs[count + size:]
        step = pl.program_id(0)
        if halves:
            wh_ref, wl_ref, keep, send, near, far, ah_ref, al_ref, gh_ref, gl_ref, high, low, gh, gl, sems = refs
            wh, wl = wh_ref[...], wl_ref[...]
        else:
            w_ref, keep, send, near, far, ah_ref, al_ref, gh_ref, gl_ref, wh_ref, wl_ref, high, low, gh, gl, sems = refs
            wh, wl = split(w_ref[...])
            wh_ref[...] = wh
            wl_ref[...] = wl

        def source(k):
            return pl.ds(order.index(k) * block, block)

        def copies():
            return copies_out(high, low, ah_ref, al_ref, sems, count, block, source)

        @pl.when(step == 0)
        def _():
            for k in range(count):
                high[source(k), :], low[source(k), :] = split(ins[k][...])
            for copy in copies():
                copy.start()
            near[...] = jnp.zeros_like(near)
            far[...] = jnp.zeros_like(far)

        for k in range(size):
            h, l = split(grads[k][...])
            gh_ref[k * block:(k + 1) * block, :] = h
            gl_ref[k * block:(k + 1) * block, :] = l
            at = pl.ds(pl.multiple_of(placed(s_ref[2], size, k) * block, block), block)
            gh[at, :] = h
            gl[at, :] = l
        out = three_passes(high[...], low[...], wh, wl, 1, 0)
        keep[...] = out[:half]
        send[...] = out[half:]
        part = three_passes(gh[...], gl[...], wh, wl, 1, 1)
        near[...] += part[:some]
        far[...] += part[some:]

        @pl.when(step == steps - 1)
        def _():
            for copy in copies():
                copy.wait()

    def column(extent):
        return pl.BlockSpec((extent, tile), lambda i, s: (0, i))

    anywhere = pl.BlockSpec(memory_space=pl.ANY)
    whole = pl.BlockSpec((some, depth), lambda i, s: (0, 0))
    given, extra = (list(weight), 0) if halves else ([weight], 2)
    boxed = [pltpu.VMEM((len(flat), block, depth), jnp.float32)] + [pltpu.SemaphoreType.DMA((len(flat),))] * 2
    held_in = [source_of] if flat else []
    return call(kernel, (steps,),
                [anywhere] * len(held_in) + specs + [column(block)] * size + [column(depth)] * len(given),
                [column(half)] * 2 + [whole] * 2 + [anywhere] * 2 + [column(size * block)] * 2 + [column(depth)] * extra
                + [anywhere] * len(others),
                [f32(half, width)] * 2 + [f32(some, depth)] * 2 + [bf16(count * block, depth)] * 2
                + [bf16(size * block, width)] * 2 + [bf16(depth, width)] * extra
                + [f32(len(rows_of) * block, depth) for _, rows_of in others],
                [pltpu.VMEM((count * block, depth), jnp.bfloat16)] * 2
                + [pltpu.VMEM((size * block, tile), jnp.bfloat16)] * 2 + [pltpu.SemaphoreType.DMA((2, count))]
                + (boxed if flat else []),
                scalars, held_in + rows + group + given, 6 * (count + size) * block * depth * width)


def backward(scalars, groups, weight, block, beside=()):
    depth, width = weight[0].shape
    size = len(groups[0])
    count = size * len(groups)
    tile = tile_of(depth, 256)
    half = size // 2 * block
    steps = depth // tile
    parts = 2 * len(groups)

    def kernel(s_ref, *refs):
        ins, wh_ref, wl_ref = refs[:count], refs[count], refs[count + 1]
        if beside:
            refs[-4][...] = refs[count + 2][...] + refs[count + 3][...]
            refs = refs[:count + 2] + refs[count + 4:-4] + refs[-3:]
        outs = refs[count + 2:count + 2 + parts]
        out_h, out_l, high, low, sems = refs[count + 2 + parts:]

        def source(k):
            return pl.ds(pl.multiple_of(placed(s_ref[2], size, k) * block, block), block)

        def copies():
            return copies_out(high, low, out_h, out_l, sems, count, block, source)

        @pl.when(pl.program_id(0) == 0)
        def _():
            for k in range(count):
                high[source(k), :], low[source(k), :] = split(ins[k][...])
            for copy in copies():
                copy.start()

        out = three_passes(high[...], low[...], wh_ref[...], wl_ref[...], 1, 1)
        for k in range(parts):
            outs[k][...] = out[k * half:(k + 1) * half]

        @pl.when(pl.program_id(0) == steps - 1)
        def _():
            for copy in copies():
                copy.wait()

    flat = [g for group in groups for g in group]
    anywhere = pl.BlockSpec(memory_space=pl.ANY)
    part = pl.BlockSpec((half, tile), lambda i, s: (0, i))
    row = pl.BlockSpec((tile, width), lambda i, s: (i, 0))
    wide = width // steps
    return call(kernel, (steps,),
                [once((block, width), lambda i, s: (0, 0)) for _ in flat] + [row, row]
                + [pl.BlockSpec((block, wide), lambda i, s: (1, i))] * len(beside),
                [part] * parts + [anywhere, anywhere] + [pl.BlockSpec((block, wide), lambda i, s: (0, i))] * (len(beside) // 2),
                [f32(half, depth)] * parts + [bf16(count * block, width)] * 2 + [f32(block, width)] * (len(beside) // 2),
                [pltpu.VMEM((count * block, width), jnp.bfloat16)] * 2 + [pltpu.SemaphoreType.DMA((2, count))],
                scalars, flat + list(weight) + list(beside), 6 * count * block * depth * width)


def cuts(extent, twelfths=5):
    at = extent * twelfths // 12 // 128 * 128
    return [slice(0, at), slice(at, extent)] if at else [slice(0, extent)]


def total_of(scalars, base, chunks, block):
    width = base.shape[1]
    columns = cuts(width, 9)
    flat = [c for part in chunks for c in part]

    def kernel(s_ref, *refs):
        base_ref, ins, out = refs[0], refs[1:-1], refs[-1]
        for c, at in enumerate(columns):
            total = base_ref[:, at]
            for k in range(len(chunks)):
                total = total + ins[k * len(columns) + c][...]
            out[:, at] = total

    whole = pl.BlockSpec((block, width), lambda i, s: (0, 0))
    return call(kernel, (1,), [whole] + [pl.BlockSpec(c.shape, lambda i, s: (0, 0)) for c in flat],
                whole, f32(block, width), [], scalars, [base] + flat, 0)


def slabs_of(scalars, own, slabs, block, depth):
    toks = len(slabs)
    columns = cuts(depth)
    flat = [piece for pieces in slabs[1:] for piece in pieces]

    def theirs(s_ref, *refs):
        ins, out = refs[:-2], refs[-1]
        for s in range(toks - 1):
            @pl.when(pl.program_id(0) == s)
            def _():
                for c, at in enumerate(columns):
                    out[:, at] = ins[s * len(columns) + c][...]

    return call(theirs, (toks - 1,),
                [pl.BlockSpec(a.shape, lambda i, s: (0, 0)) for a in flat] + [pl.BlockSpec(memory_space=pl.ANY)],
                pl.BlockSpec((block, depth), lambda i, s: (0, s[1] ^ (i + 1))), f32(block, toks * depth), [], scalars,
                flat + [own], 0, {len(flat) + 1: 0})


def weight_rows(scalars, acts, grads, first, count, depth, width, before, sums=()):
    tile = tile_of(width, 512)
    n, m = len(acts), len(grads)

    def kernel(s_ref, *refs):
        def joined(part):
            return jnp.concatenate([ref[...] for ref in part], 0)

        lh, ll = joined(refs[:n]), joined(refs[n:2 * n])
        rh, rl = joined(refs[2 * n:2 * n + m]), joined(refs[2 * n + m:2 * n + 2 * m])
        outs = refs[len(refs) - 1 - len(sums):]
        outs[0][...] = three_passes(lh, ll, rh, rl, 0, 0)
        at = given
        for out, (arrays, *_) in zip(outs[1:], sums):
            total = refs[at][...]
            for k in range(1, len(arrays)):
                total = total + refs[at + k][...]
            out[...] = total
            at += len(arrays)

    args = [a[0] for a in acts] + [a[1] for a in acts] + [g[0] for g in grads] + [g[1] for g in grads]
    specs = [once((a.shape[0], count), lambda i, s: (0, first)) for a in args[:2 * n]]
    specs += [pl.BlockSpec((g.shape[0], tile), lambda i, s: (0, i)) for g in args[2 * n:]]
    aliases, tokens = None, sum(a[0].shape[0] for a in acts)
    if before is not None:
        args.append(before)
        specs.append(pl.BlockSpec(memory_space=pl.ANY))
        aliases = {len(args): 0}
    given, steps = len(args), width // tile
    out_specs, out_shape = [pl.BlockSpec((count, tile), lambda i, s: (first, i))], [f32(depth, width)]
    for arrays, rows, extent, whole, place in sums:
        args += arrays
        specs += [pl.BlockSpec((rows, extent // steps), lambda i, s: (0, i))] * len(arrays)
        out_specs.append(pl.BlockSpec((rows, extent // steps), functools.partial(lambda p, i, s: (0, p(s) * steps + i), place)))
        out_shape.append(f32(rows, whole))
    return call(kernel, (steps,), specs, out_specs, out_shape, [], scalars, args, 6 * count * width * tokens, aliases)


def halved(keep, send, axis, levels):
    for k, bit in enumerate(levels):
        if k:
            half = keep.shape[0] // 2
            keep, send = keep[:half], keep[half:]
        keep = keep + swap(send, axis, bit)
    return keep


def halved_to(keep, send, axis, levels):
    total = halved(keep, send, axis, levels)
    half = total.shape[0] // 2
    return total[:half], total[half:]


def shards(acts, weight, grad_out):
    toks, fins, fouts = (lax.axis_size(name) for name in ("tok", "fin", "fout"))
    tok, fin, fout = (lax.axis_index(name) for name in ("tok", "fin", "fout"))
    block = grad_out.shape[0]
    depth, width = weight.shape
    scalars = jnp.stack([fin, tok, fin ^ fout])
    top = fins // 2
    order = mirrored(fins)
    low = mirrored(top)

    held = {(0, 0): grad_out}
    for bit in bits(toks):
        held.update({(s ^ bit, r): swap(v, "tok", bit) for (s, r), v in held.items()})
    for bit in reversed(bits(fins)):
        held.update({(s, r ^ bit): swap(v, "fin", bit) for (s, r), v in held.items()})

    def columns(s):
        if depth % 128 == 0:
            return acts, lambda sc: sc[1] ^ s
        return lax.dynamic_slice(acts, (0, (tok ^ s) * depth), (acts.shape[0], depth)), lambda sc: 0

    lower, upper = list(range(top)), list(range(top, fins))
    rows, others = {}, []
    for s in range(1, toks):
        for tag, part in (("u", upper), ("l", lower)):
            if depth % 128 == 0:
                others.append((s, part))
            else:
                rows[s, tag] = jnp.concatenate(
                    [lax.dynamic_slice(acts, ((fin ^ r) * block, (tok ^ s) * depth), (block, depth)) for r in part], 0)

    source, column = columns(0)
    specs = [once((block, depth), functools.partial(lambda r, i, s: (s[0] ^ r, column(s)), r)) for r in range(fins)]
    keep, send, near, far, ah, al, gh, gl, wh, wl, *packed = first(
        scalars, [source] * fins, specs, order, [held[0, r] for r in lower], weight, block,
        acts, lambda s, sc: sc[1] ^ s, others)
    weight = wh, wl
    for (s, part), array in zip(others, packed):
        rows[s, "l" if part is lower else "u"] = array
    rows = {(s, tag): swap(array, "tok", s) for (s, tag), array in rows.items()}
    acts_of, grads_of = [(ah, al)], [(gh, gl)]
    partial = {(0, "a"): halved(near, far, "fout", bits(fouts)[:-1])}
    levels = bits(fins)
    if len(levels) > 2:
        keep, send = halved_to(keep, send, "fin", levels[:-2])
    moved = swap(send, "fin", levels[-2])
    theirs = None

    groups = []
    for s in range(1, toks):
        groups += [(f"pb{s - 1}", [(s - 1, upper)]), (f"pa{s}", [(s, lower)])]
    for name, members in groups:
        aside = name == "pa1" and width // (depth // tile_of(depth, 256)) % 128 == 0
        outs = backward(scalars, [[held[s, r] for r in part] for s, part in members], weight, block,
                        (keep, moved) if aside else ())
        at = 2 * len(members)
        grads_of.append((outs[at], outs[at + 1]))
        theirs = outs[at + 2] if aside else theirs
        for k, (s, part) in enumerate(members):
            tag = "a" if part is lower else "b"
            partial[s, tag] = halved(outs[2 * k], outs[2 * k + 1], "fout", bits(fouts)[:-1])

    if theirs is None:
        theirs = keep[block:] + moved[block:]
    own = swap(theirs, "fin", top)
    parts = []
    for s in range(1, toks):
        done = {}
        for tag in ("u", "l"):
            pieces = [rows[s, tag]] * top
            specs = [once((block, depth), functools.partial(lambda k, i, s: (k, 0), k)) for k in range(top)]
            if tag == "u" and s == toks - 1:
                keep_u, send_u, near, far, ah, al, gh, gl = first(
                    scalars, pieces, specs, low, [held[s, r] for r in upper], weight, block)
                done[tag] = keep_u, send_u, ah, al
                grads_of.append((gh, gl))
                partial[s, "b"] = halved(near, far, "fout", bits(fouts)[:-1])
            else:
                done[tag] = forward(scalars, pieces, specs, low, weight, block)
        keep_u, send_u = done["u"][:2]
        if len(levels) > 2:
            keep_u, send_u = halved_to(keep_u, send_u, "fin", levels[:-2])
        moved_u = swap(send_u, "fin", levels[-2])
        down = halved(done["l"][0], done["l"][1], "fin", levels[:-1])
        acts_of += [done["l"][2:], done["u"][2:]]
        chunks = []
        for cols in cuts(width, 9):
            chunk = down[:, cols] + swap(keep_u[:, cols] + moved_u[:, cols], "fin", top)
            chunks.append(swap(chunk, "tok", s))
        parts.append(chunks)
    kept_rows = [keep, moved, own]
    upper_first = (((fin ^ fout) // top) & 1) == 1
    slabs = []
    for s in range(toks):
        a, b = partial[s, "a"], partial[s, "b"]
        keep, send = jnp.where(upper_first, b, a), jnp.where(upper_first, a, b)
        if s == 0:
            slabs.append([(keep, swap(send, "fout", fouts // 2))])
            continue
        pieces = []
        for cols in cuts(depth):
            piece = keep[:, cols] + swap(send[:, cols], "fout", fouts // 2)
            pieces.append(swap(piece, "tok", s))
        slabs.append(pieces)
    grad_weight = None
    third = depth // 3
    pieces = [(0, 2 * third), (2, third)] if depth % 384 == 0 else [(0, depth)]
    steps = width // tile_of(width, 512)
    sums = [(kept_rows, block, width, width, lambda sc: 0)]
    apart = depth % (128 * steps) == 0
    if apart:
        sums.append((list(slabs[0][0]), block, depth, toks * depth, lambda sc: sc[1]))
    for c, (start, count) in enumerate(pieces):
        last = c == len(pieces) - 1
        grad_weight, *added = weight_rows(scalars, acts_of, grads_of, start, count, depth, width, grad_weight,
                                          sums if last else ())
    outputs = total_of(scalars, added[0], parts, block)
    if apart:
        grad_acts = slabs_of(scalars, added[1], slabs, block, depth)
    else:
        grad_acts = jnp.zeros((block, depth * toks), jnp.float32)
        for s in range(toks):
            slab = sum(slabs[s][0]) if s == 0 else jnp.concatenate(slabs[s], 1)
            grad_acts = lax.dynamic_update_slice(grad_acts, slab, (0, (tok ^ s) * depth))
    return outputs, grad_acts, grad_weight


def solution(mesh):
    in_specs = (P("tok", "fin"), P(("fin", "tok"), "fout"), P(("tok", "fin"), "fout"))
    out_specs = (P(("tok", "fin"), "fout"), P(("tok", "fout"), "fin"), P(("fin", "tok"), "fout"))

    return jax.shard_map(shards, mesh=mesh, in_specs=in_specs, out_specs=out_specs, check_vma=False)
```
